512 devices in a mesh: coef: 16 (over z_lo, y), pair: 32 (over z_hi, x, core).
Axes of the slice: x: 4, y: 4, z: 16 (z_hi: 4, z_lo: 4; z = z_hi * 4 + z_lo), core: 2. Of those that a mesh axis runs over, the one named last changes fastest.
Arguments:
- integrals: bfloat16 [2048, 32, 8192], P(('coef', 'pair')), may hold values from -66 to 66
- coefficients: bfloat16 [2, 8192, 384], P(None, ('coef', 'pair')), may hold values from -0.0625 to 0.0625
- shell_starts: int32 [8], replicated, may hold values from 0 to 8188, as said below
- pair_ids: int32 [16, 128], P('coef'), may hold values from 0 to 127, each once within a row
Outputs:
- half_ints: bfloat16 [2, 384, 384, 2048], P(None, 'pair', None, 'coef')
The draws below stay inside these ranges and needn't reach their ends.
Inputs may be any that keep to these rules, and one draw needn't show every extreme that they name: `shell_starts`: distinct multiples of 4.
All inputs are finite; a program needn't handle non-finite values.
Results may differ from the reference program's by a relative error of at most 0.0049.
Values may be sent and summed in bfloat16 or wider, within the bound.
A program may use at most 64 MiB of HBM per device.

```python
import jax
import jax.numpy as jnp
from jax import lax

NAO = 8192
NOCC = 384
SHW = 4
BS = 8
MB = 32
KP_COEF = 128
KPAIRS = 2048
N_COEF = 16


def draw_shell_starts(key, part):
    total_shells = NAO // SHW
    middle = jax.random.permutation(jax.random.fold_in(key, 11), total_shells - 2)[:BS - 2] + 1
    ends = jnp.array([0, total_shells - 1], dtype=jnp.int32)
    chosen = jnp.concatenate([ends, middle.astype(jnp.int32)])
    order = jax.random.permutation(jax.random.fold_in(key, 12), BS)
    return (chosen[order] * SHW).astype(jnp.int32)


def levels(stream_key, dims, split, low, top_value):
    loudness, own = 1.0, jax.random.fold_in(stream_key, 6)
    for dim, parts in split:
        draws = jnp.exp(jax.random.uniform(jax.random.fold_in(own, dim), (parts,), jnp.float32, low / len(split), top_value / len(split)))
        loudness = loudness * jnp.repeat(draws, dims[dim] // parts).reshape([-1 if axis == dim else 1 for axis in range(len(dims))])
    return loudness


def noise(own_key, extent, width, most, split=(), kind=jnp.bfloat16):
    values = width * jax.random.normal(own_key, extent, jnp.float32)
    if split:
        values = values * levels(own_key, extent, split, -0.22, 0.18)
    return jnp.clip(values, -most, most).astype(kind)


def setup_inputs(seed: int = 0) -> dict:
    streams_of = jax.random.split(jax.random.key(seed), 5)
    integrals = noise(streams_of[0], (KPAIRS, MB, NAO), 11.0, 66.0, ((0, 512),))
    coefficients = noise(streams_of[1], (2, NAO, NOCC), NAO ** -0.5, 0.0625, ((1, 512),))
    shell_starts = draw_shell_starts(jax.random.fold_in(streams_of[4], 71), 0)
    pair_ids = jax.vmap(lambda own: jax.random.permutation(own, KP_COEF))(jax.random.split(streams_of[3], N_COEF)).reshape((N_COEF, KP_COEF)).astype(jnp.int32)
    return dict(integrals=integrals, coefficients=coefficients, shell_starts=shell_starts, pair_ids=pair_ids)


def reference(integrals, coefficients, shell_starts, pair_ids):
    offsets = jnp.arange(SHW, dtype=jnp.int32)
    batch_index = (shell_starts[:, None] + offsets[None, :]).reshape(-1).astype(jnp.int32)
    batch_coef = jnp.take(coefficients, batch_index, axis=1)
    coef_real = batch_coef[0].astype(jnp.float32)
    coef_imag = batch_coef[1].astype(jnp.float32)
    blocks = integrals.reshape(N_COEF, KP_COEF * MB, NAO)

    def transform(pair_item):
        int_block, pair_order = pair_item
        half_real = jnp.dot(int_block, coefficients[0], preferred_element_type=jnp.float32).astype(jnp.bfloat16)
        half_imag = jnp.dot(int_block, coefficients[1], preferred_element_type=jnp.float32).astype(jnp.bfloat16)
        half_real = half_real.reshape(KP_COEF, MB, NOCC).astype(jnp.float32)
        half_imag = half_imag.reshape(KP_COEF, MB, NOCC).astype(jnp.float32)
        real_part = jnp.einsum("mi,kmj->kij", coef_real, half_real) + jnp.einsum("mi,kmj->kij", coef_imag, half_imag)
        imag_part = jnp.einsum("mi,kmj->kij", coef_real, half_imag) - jnp.einsum("mi,kmj->kij", coef_imag, half_real)
        stacked = jnp.stack([real_part, imag_part]).astype(jnp.bfloat16)
        placed = jnp.zeros((2, KP_COEF, NOCC, NOCC), jnp.bfloat16).at[:, pair_order].set(stacked)
        return placed

    result = lax.map(transform, (blocks, pair_ids))
    return jnp.transpose(result, (1, 3, 4, 0, 2)).reshape(2, NOCC, NOCC, N_COEF * KP_COEF)
```

```python
import jax
import jax.numpy as jnp
from jax import lax
from jax.experimental import pallas as pl
from jax.experimental.pallas import tpu as pltpu
from jax.sharding import PartitionSpec as P

MESH = pl.DeviceIdType.MESH
SHW = 4
F32 = jnp.float32
BF16 = jnp.bfloat16


def kernel(starts_ref, order_ref, ints_ref, coef_ref, out_ref,
           rows, panel, half, batch, mix, trans, outv,
           loc_sem, cc_s, cc_r, ci_s, ci_r, ring_s, ring_r, fx_s, fx_r, fy_s, fy_r, fz_s, fz_r,
           mid_s, mid_r, midf_s, midf_r, last_s, last_r, lastf_s, lastf_r,
           b_s, b_r, hz_s, hz_r, hzf_s, hzf_r, hx_s, hx_r, hxf_s, hxf_r, hp_s, hp_r):
    a = lax.axis_index("coef")
    p = lax.axis_index("pair")
    zlo, y = a // 4, a % 4
    zhi, x, c = p // 8, (p // 2) % 4, p % 2
    z = zhi * 4 + zlo
    other = 1 - c

    def dev(z_, y_, x_, c_):
        return ((z_ % 4) * 4 + y_, (z_ // 4) * 8 + x_ * 2 + c_)

    def zz(k):
        return (z + k + 16) % 16

    def yy(k):
        return (y + k + 4) % 4

    def xx(k):
        return (x + k + 4) % 4

    def hh(k):
        return (zhi + k + 4) % 4

    partner = dev(z, y, x, other)
    z_to = (dev(zz(1), y, x, c), dev(zz(-1), y, x, c))
    y_to = (dev(z, yy(1), x, c), dev(z, yy(-1), x, c))
    x_to = (dev(z, y, xx(1), c), dev(z, y, xx(-1), c))
    h_to = (dev(zz(4), y, x, c), dev(zz(-4), y, x, c))
    y_far = dev(z, yy(2), x, c)
    x_far = dev(z, y, xx(2), c)
    SIGN = (1, -1)

    def remote(ref, ssem, rsem, to):
        return pltpu.make_async_remote_copy(src_ref=ref, dst_ref=ref, send_sem=ssem, recv_sem=rsem,
                                            device_id=to, device_id_type=MESH)

    core_rows = pl.ds(pl.multiple_of(c * 16, 16), 16)
    int_rows = pl.ds(pl.multiple_of(c * 128, 128), 128)

    def own_coef(j):
        return pltpu.make_async_copy(coef_ref.at[c, :, pl.ds(128 * j, 128)],
                                     panel.at[j, zlo, y, zhi, x, core_rows, :], loc_sem.at[j])

    own_ints = pltpu.make_async_copy(ints_ref, rows.at[int_rows, :], loc_sem.at[3])

    def give_coef(j):
        return pltpu.make_async_remote_copy(
            src_ref=coef_ref.at[other, :, pl.ds(128 * j, 128)],
            dst_ref=panel.at[j, zlo, y, zhi, x, core_rows, :],
            send_sem=cc_s.at[j], recv_sem=cc_r.at[j], device_id=partner, device_id_type=MESH)

    def got_coef(j):
        ref = panel.at[j, zlo, y, zhi, x, pl.ds(pl.multiple_of(other * 16, 16), 16), :]
        return remote(ref, cc_s.at[j], cc_r.at[j], partner)

    give_ints = pltpu.make_async_remote_copy(
        src_ref=ints_ref, dst_ref=rows.at[int_rows, :],
        send_sem=ci_s.at[0], recv_sem=ci_r.at[0], device_id=partner, device_id_type=MESH)
    got_ints = remote(rows.at[pl.ds(pl.multiple_of(other * 128, 128), 128), :], ci_s.at[0], ci_r.at[0], partner)

    for j in (2, 0, 1):
        own_coef(j).start()
    own_ints.start()

    barrier = pltpu.get_barrier_semaphore()
    peers = (partner,) + z_to + y_to + x_to + h_to + (y_far, x_far)
    for peer in peers:
        pl.semaphore_signal(barrier, inc=1, device_id=peer, device_id_type=MESH)
    pl.semaphore_wait(barrier, len(peers))

    for j in (2, 0, 1):
        give_coef(j).start()
    give_ints.start()

    def ring(n, d, j, back):
        o = (z - SIGN[n] * (d - back) + 32) % 16
        return remote(panel.at[j, o % 4, y, o // 4, x], ring_s.at[n, d, j], ring_r.at[n, d, j], z_to[n])

    def fanx(k, back):
        to = (x_to[0], x_far, x_to[1])[k - 1]
        return remote(panel.at[2, zlo, y, zhi, xx(-k * (1 - back))], fx_s.at[k], fx_r.at[k], to)

    def fany(k, back):
        to = (y_to[0], y_far, y_to[1])[k - 1]
        return remote(panel.at[2, zlo, yy(-k * (1 - back)), zhi], fy_s.at[k], fy_r.at[k], to)

    def fanz(n, d, w, back):
        o = (z - SIGN[n] * (d - back) + 32) % 16
        return remote(panel.at[2, o % 4, w, o // 4], fz_s.at[n, d, w], fz_r.at[n, d, w], z_to[n])

    def ring_step(d, final=False):
        for n in range(2):
            for j in range(2):
                ring(n, d, j, 0).wait_recv()
                if not final or n == j:
                    ring(n, d + 1, j, 1).start()

    def fanz_step(d, final=False):
        for w in range(4):
            for n in range(2):
                fanz(n, d, w, 0).wait_recv()
                if not final or n == w // 2:
                    fanz(n, d + 1, w, 1).start()

    for j in (2, 0, 1):
        own_coef(j).wait()
        got_coef(j).wait_recv()
        if j == 2:
            for k in (1, 3, 2):
                fanx(k, 1).start()
        else:
            for n in range(2):
                ring(n, 1, j, 1).start()

    lane = lax.broadcasted_iota(jnp.int32, (32, 512), 1)
    row = lax.broadcasted_iota(jnp.int32, (32, 512), 0)
    want = row % SHW
    for s in range(8):
        want = want + jnp.where(row // SHW == s, starts_ref[s], 0)

    def pick(q, carry):
        at = pl.multiple_of(q * 512, 512)
        rows[256:288, pl.ds(at, 512)] = jnp.where(lane + q * 512 == want, 1.0, 0.0).astype(BF16)
        return carry

    ring_step(1)
    for k in (1, 3, 2):
        fanx(k, 0).wait_recv()
    for k in (1, 3, 2):
        fany(k, 1).start()
    lax.fori_loop(0, 16, pick, 0)
    ring_step(2)
    ring_step(3)

    def more(d, carry):
        ring_step(d)
        return carry

    lax.fori_loop(4, 7, more, 0)
    ring_step(7, True)
    for k in (1, 3, 2):
        fany(k, 0).wait_recv()
    for w in range(4):
        for n in range(2):
            fanz(n, 1, w, 1).start()
    for n in range(2):
        ring(n, 8, n, 0).wait_recv()

    def spot(ch, m, l):
        return (l, m) if ch == 0 else (m, l)

    mid_to = (x_to, y_to)
    last_to = (y_to, x_to)
    here = (x, y)
    line = (y, x)

    def wrap(v, k):
        return (v + k + 4) % 4

    def mid(ch, n, back):
        y_, x_ = spot(ch, wrap(here[ch], -SIGN[n] * (1 - back)), line[ch])
        return remote(panel.at[ch, :, y_, :, x_], mid_s.at[ch, n], mid_r.at[ch, n], mid_to[ch][n])

    def midf(ch, n, back):
        y_, x_ = spot(ch, wrap(here[ch], -SIGN[n] * (2 - back)), line[ch])
        return remote(panel.at[ch, pl.ds(2 * n, 2), y_, :, x_], midf_s.at[ch, n], midf_r.at[ch, n], mid_to[ch][n])

    def last(ch, k, n, back):
        y_, x_ = spot(ch, wrap(here[ch], k), wrap(line[ch], -SIGN[n] * (1 - back)))
        return remote(panel.at[ch, :, y_, :, x_], last_s.at[ch, k, n], last_r.at[ch, k, n], last_to[ch][n])

    def lastf(ch, k, n, back):
        y_, x_ = spot(ch, wrap(here[ch], k), wrap(line[ch], -SIGN[n] * (2 - back)))
        return remote(panel.at[ch, pl.ds(2 * n, 2), y_, :, x_], lastf_s.at[ch, k, n], lastf_r.at[ch, k, n],
                      last_to[ch][n])

    def last_go(k):
        for ch in range(2):
            for n in range(2):
                last(ch, k, n, 1).start()

    def last_on(k):
        for ch in range(2):
            for n in range(2):
                last(ch, k, n, 0).wait_recv()
                lastf(ch, k, n, 1).start()

    for ch in range(2):
        for n in range(2):
            mid(ch, n, 1).start()
    last_go(0)
    fanz_step(1)
    for ch in range(2):
        for n in range(2):
            mid(ch, n, 0).wait_recv()
            midf(ch, n, 1).start()
    last_go(1)
    last_go(3)
    fanz_step(2)
    for ch in range(2):
        for n in range(2):
            midf(ch, n, 0).wait_recv()
    last_go(2)
    fanz_step(3)
    last_on(0)
    fanz_step(4)
    last_on(1)
    fanz_step(5)
    last_on(3)
    fanz_step(6)
    last_on(2)
    fanz_step(7, True)
    own_ints.wait()
    got_ints.wait_recv()
    for w in range(4):
        fanz(w // 2, 8, w, 0).wait_recv()

    def piece(j, c_, x_, h_):
        return half.at[j, c_, x_, h_]

    def part(j, c_, x_, h_, n):
        return half.at[j, c_, x_, h_, pl.ds(128 * n, 128), :]

    def hz(j, n, back):
        return remote(piece(j, c, x, hh(-SIGN[n] * (1 - back))), hz_s.at[j, n], hz_r.at[j, n], h_to[n])

    def hzf(j, n, back):
        return remote(part(j, c, x, hh(-SIGN[n] * (2 - back)), n), hzf_s.at[j, n], hzf_r.at[j, n], h_to[n])

    def hx(j, k, n, back):
        return remote(piece(j, c, xx(-SIGN[n] * (1 - back)), hh(k)), hx_s.at[j, k, n], hx_r.at[j, k, n], x_to[n])

    def hxf(j, k, n, back):
        return remote(part(j, c, xx(-SIGN[n] * (2 - back)), hh(k), n), hxf_s.at[j, k, n], hxf_r.at[j, k, n], x_to[n])

    def hp(j, xk, k, c_):
        return remote(piece(j, c_, xx(xk), hh(k)), hp_s.at[j, xk, k], hp_r.at[j, xk, k], partner)

    def contract(j):
        def step(q, acc):
            at = pl.multiple_of(q * 512, 512)
            block = panel[j, q // 4, q % 4].reshape(512, 128)
            return acc + jnp.dot(rows[:, pl.ds(at, 512)], block, preferred_element_type=F32)

        acc = lax.fori_loop(0, 16, step, jnp.zeros((288, 128), F32))
        half[j, c, x, zhi] = acc[:256].astype(BF16)
        batch[c, :, 128 * j:128 * (j + 1)] = acc[256:].astype(BF16)

    def spread(j, k):
        for n in range(2):
            hx(j, k, n, 1).start()
        hp(j, 0, k, c).start()

    def e0(j):
        for n in range(2):
            hz(j, n, 1).start()
        spread(j, 0)

    def e1(j):
        for n in range(2):
            hz(j, n, 0).wait_recv()
            hzf(j, n, 1).start()
        spread(j, 1)
        spread(j, 3)

    def e2(j):
        for n in range(2):
            hzf(j, n, 0).wait_recv()
        spread(j, 2)

    def x1(j, k):
        for n in range(2):
            hx(j, k, n, 0).wait_recv()
            hxf(j, k, n, 1).start()
        hp(j, 3, k, c).start()
        hp(j, 1, k, c).start()

    def x2(j, k):
        for n in range(2):
            hxf(j, k, n, 0).wait_recv()
        hp(j, 2, k, c).start()

    contract(2)
    e0(2)
    for k in (0, 1, 3, 2):
        for ch in range(2):
            for n in range(2):
                lastf(ch, k, n, 0).wait_recv()
    contract(0)
    e0(0)
    contract(1)
    e0(1)
    swap = remote(batch.at[c], b_s.at[0], b_r.at[0], partner)
    swap.start()

    J = (2, 0, 1)
    for j in J:
        x1(j, 0)
    remote(batch.at[other], b_s.at[0], b_r.at[0], partner).wait_recv()

    r96 = lax.broadcasted_iota(jnp.int32, (96, 384), 0)
    c384 = lax.broadcasted_iota(jnp.int32, (96, 384), 1)
    chosen = jnp.where(c384 == p * 12 + r96 // 8, 1.0, 0.0).astype(BF16)
    r256 = lax.broadcasted_iota(jnp.int32, (96, 256), 0)
    c256 = lax.broadcasted_iota(jnp.int32, (96, 256), 1)
    same = r256 % 8 == c256 // 32
    grid = []
    for t in range(2):
        wide = jnp.concatenate([batch[t]] * 8, axis=0)
        g = lax.dot_general(chosen, wide, (((1,), (1,)), ((), ())), preferred_element_type=F32)
        grid.append(jnp.where(same, g, 0.0))
    mix[0:96, 0:256] = grid[0].astype(BF16)
    mix[0:96, 256:512] = grid[1].astype(BF16)
    mix[96:192, 0:256] = (-grid[1]).astype(BF16)
    mix[96:192, 256:512] = grid[0].astype(BF16)
    spots = lax.broadcasted_iota(jnp.int32, (128, 128), 0)
    select = jnp.transpose(jnp.where(spots == order_ref[0:1, :], 1.0, 0.0)).astype(BF16)

    for j in J:
        x2(j, 0)
    e1(2)
    for k in (1, 3):
        x1(2, k)
    e1(0)
    for k in (1, 3):
        x2(2, k)
    for k in (1, 3):
        x1(0, k)
    e1(1)
    for k in (1, 3):
        x2(0, k)
    for k in (1, 3):
        x1(1, k)
    e2(2)
    for k in (1, 3):
        x2(1, k)
    x1(2, 2)
    e2(0)
    x2(2, 2)
    x1(0, 2)
    e2(1)
    x2(0, 2)
    x1(1, 2)
    x2(1, 2)

    def mixed(j):
        for xk in range(4):
            for k in range(4):
                hp(j, xk, k, other).wait_recv()

        def one(t, carry):
            h_, x_ = t // 4, t % 4
            v = jnp.dot(mix[:, 0:256], half[j, 0, x_, h_], preferred_element_type=F32)
            v = v + jnp.dot(mix[:, 256:512], half[j, 1, x_, h_], preferred_element_type=F32)
            trans[:, pl.ds(pl.multiple_of(t * 8, 8), 8), :] = v.reshape(24, 8, 128)
            return carry

        lax.fori_loop(0, 16, one, 0)

        def turn(t, carry):
            v = jnp.transpose(trans[t]).astype(BF16)
            outv[t, 128 * j:128 * (j + 1), :] = jnp.dot(v, select, preferred_element_type=F32).astype(BF16)
            return carry

        lax.fori_loop(0, 24, turn, 0)

    def put(j):
        cols = pl.ds(128 * j, 128)
        return pltpu.make_async_copy(outv.at[:, cols, :], out_ref.at[:, cols, :], loc_sem.at[j])

    for j in J:
        mixed(j)
        put(j).start()

    for j in range(3):
        give_coef(j).wait_send()
    give_ints.wait_send()
    swap.wait_send()
    for k in (1, 2, 3):
        fanx(k, 1).wait_send()
        fany(k, 1).wait_send()

    def drain(d, carry):
        for n in range(2):
            for j in range(2):
                ring(n, d, j, 1).wait_send()
            for w in range(4):
                fanz(n, d, w, 1).wait_send()
        return carry

    lax.fori_loop(1, 8, drain, 0)
    for n in range(2):
        ring(n, 8, n, 1).wait_send()
    for w in range(4):
        fanz(w // 2, 8, w, 1).wait_send()
    for n in range(2):
        for ch in range(2):
            mid(ch, n, 1).wait_send()
            midf(ch, n, 1).wait_send()
            for k in range(4):
                last(ch, k, n, 1).wait_send()
                lastf(ch, k, n, 1).wait_send()
        for j in range(3):
            hz(j, n, 1).wait_send()
            hzf(j, n, 1).wait_send()
            for k in range(4):
                hx(j, k, n, 1).wait_send()
                hxf(j, k, n, 1).wait_send()
    for j in range(3):
        for xk in range(4):
            for k in range(4):
                hp(j, xk, k, c).wait_send()
    for j in range(3):
        put(j).wait()


def on_device(integrals, coefficients, shell_starts, pair_ids):
    slot_count, batch_rows, ao_width = integrals.shape
    ints = integrals.reshape(slot_count * batch_rows, ao_width)
    D = pltpu.SemaphoreType.DMA
    pairs = [(3,), (1,), (2, 9, 2), (4,), (4,), (2, 9, 4), (2, 2), (2, 2), (2, 4, 2), (2, 4, 2),
             (1,), (3, 2), (3, 2), (3, 4, 2), (3, 4, 2), (3, 4, 4)]
    sems = [D((4,))]
    for shape in pairs:
        sems += [D(shape), D(shape)]
    out = pl.pallas_call(
        kernel,
        out_shape=jax.ShapeDtypeStruct((24, 384, 128), BF16),
        in_specs=[
            pl.BlockSpec(memory_space=pltpu.SMEM),
            pl.BlockSpec(memory_space=pltpu.VMEM),
            pl.BlockSpec(memory_space=pl.ANY),
            pl.BlockSpec(memory_space=pl.ANY),
        ],
        out_specs=pl.BlockSpec(memory_space=pl.ANY),
        scratch_shapes=[
            pltpu.VMEM((288, 8192), BF16),
            pltpu.VMEM((3, 4, 4, 4, 4, 32, 128), BF16),
            pltpu.VMEM((3, 2, 4, 4, 256, 128), BF16),
            pltpu.VMEM((2, 32, 384), BF16),
            pltpu.VMEM((192, 512), BF16),
            pltpu.VMEM((24, 128, 128), F32),
            pltpu.VMEM((24, 384, 128), BF16),
        ] + sems,
        compiler_params=pltpu.CompilerParams(
            collective_id=0, has_side_effects=True, vmem_limit_bytes=50 * 1024 * 1024),
    )(shell_starts, pair_ids, ints, coefficients)
    return out.reshape(2, 12, 384, 128)


def solution(mesh):
    return jax.shard_map(
        on_device,
        mesh=mesh,
        in_specs=(
            P(("coef", "pair"), None, None),
            P(None, ("coef", "pair"), None),
            P(),
            P("coef", None),
        ),
        out_specs=P(None, "pair", None, "coef"),
        check_vma=False,
    )
```

```python
import jax
import jax.numpy as jnp
from jax import lax
from jax.experimental import pallas as pl
from jax.experimental.pallas import tpu as pltpu
from jax.sharding import PartitionSpec as P

MESH = pl.DeviceIdType.MESH
SHW = 4
F32 = jnp.float32
BF16 = jnp.bfloat16


def kernel(starts_in, order_in, ints_ref, coef_ref, out_ref,
           starts_ref, order_ref, rows, panel, half, batch, mix, trans, outv, acc_ab, acc_c,
           loc_sem, cc_s, cc_r, ci_s, ci_r, ring_s, ring_r, fx_s, fx_r, fy_s, fy_r, fz_s, fz_r,
           mid_s, mid_r, midf_s, midf_r, last_s, last_r, lastf_s, lastf_r,
           b_s, b_r, hz_s, hz_r, hzf_s, hzf_r, hx_s, hx_r, hxf_s, hxf_r, hp_s, hp_r):
    a = lax.axis_index("coef")
    p = lax.axis_index("pair")
    zlo, y = a // 4, a % 4
    zhi, x, c = p // 8, (p // 2) % 4, p % 2
    z = zhi * 4 + zlo
    other = 1 - c

    def dev(z_, y_, x_, c_):
        return ((z_ % 4) * 4 + y_, (z_ // 4) * 8 + x_ * 2 + c_)

    def zz(k):
        return (z + k + 16) % 16

    def yy(k):
        return (y + k + 4) % 4

    def xx(k):
        return (x + k + 4) % 4

    def hh(k):
        return (zhi + k + 4) % 4

    partner = dev(z, y, x, other)
    z_to = (dev(zz(1), y, x, c), dev(zz(-1), y, x, c))
    z2_to = (dev(zz(2), y, x, c), dev(zz(-2), y, x, c))
    y_to = (dev(z, yy(1), x, c), dev(z, yy(-1), x, c))
    x_to = (dev(z, y, xx(1), c), dev(z, y, xx(-1), c))
    h_to = (dev(zz(4), y, x, c), dev(zz(-4), y, x, c))
    y_far = dev(z, yy(2), x, c)
    x_far = dev(z, y, xx(2), c)
    SIGN = (1, -1)

    def remote(ref, ssem, rsem, to):
        return pltpu.make_async_remote_copy(src_ref=ref, dst_ref=ref, send_sem=ssem, recv_sem=rsem,
                                            device_id=to, device_id_type=MESH)

    core_rows = pl.ds(pl.multiple_of(c * 16, 16), 16)
    int_rows = pl.ds(pl.multiple_of(c * 128, 128), 128)

    def own_coef(j):
        return pltpu.make_async_copy(coef_ref.at[c, :, pl.ds(128 * j, 128)],
                                     panel.at[j, 0, y, x, core_rows, :], loc_sem.at[j])

    own_ints = pltpu.make_async_copy(ints_ref, rows.at[int_rows, :], loc_sem.at[3])

    def give_coef(j):
        return pltpu.make_async_remote_copy(
            src_ref=coef_ref.at[other, :, pl.ds(128 * j, 128)],
            dst_ref=panel.at[j, 0, y, x, core_rows, :],
            send_sem=cc_s.at[j], recv_sem=cc_r.at[j], device_id=partner, device_id_type=MESH)

    def got_coef(j):
        ref = panel.at[j, 0, y, x, pl.ds(pl.multiple_of(other * 16, 16), 16), :]
        return remote(ref, cc_s.at[j], cc_r.at[j], partner)

    give_ints = pltpu.make_async_remote_copy(
        src_ref=ints_ref, dst_ref=rows.at[int_rows, :],
        send_sem=ci_s.at[0], recv_sem=ci_r.at[0], device_id=partner, device_id_type=MESH)
    got_ints = remote(rows.at[pl.ds(pl.multiple_of(other * 128, 128), 128), :], ci_s.at[0], ci_r.at[0], partner)

    for j in range(3):
        own_coef(j).start()
    own_ints.start()
    get_starts = pltpu.make_async_copy(starts_in, starts_ref, loc_sem.at[4])
    get_order = pltpu.make_async_copy(order_in, order_ref, loc_sem.at[5])
    get_starts.start()
    get_order.start()

    barrier = pltpu.get_barrier_semaphore()
    peers = (partner,) + z_to + z2_to + y_to + x_to + h_to + (y_far, x_far)
    for peer in peers:
        pl.semaphore_signal(barrier, inc=1, device_id=peer, device_id_type=MESH)
    pl.semaphore_wait(barrier, len(peers))

    for j in range(3):
        give_coef(j).start()
    give_ints.start()

    def slot(n, d):
        return 15 if d == 8 else (0 if d == 0 else 2 * d - 1 + n)

    def both(src, dst, ssem, rsem, to):
        return pltpu.make_async_remote_copy(src_ref=src, dst_ref=dst, send_sem=ssem, recv_sem=rsem,
                                            device_id=to, device_id_type=MESH)

    def ring(n, d):
        js = pl.ds(0, 2) if d < 8 else pl.ds(n, 1)
        src = panel.at[js, slot(n, max(d - 2, 0)), y, x]
        dst = panel.at[js, slot(n, d), y, x]
        return both(src, dst, ring_s.at[n, d], ring_r.at[n, d], (z_to if d == 1 else z2_to)[n])

    def fanx(k, back):
        to = (x_to[0], x_far, x_to[1])[k - 1]
        return remote(panel.at[2, 0, y, xx(-k * (1 - back))], fx_s.at[k], fx_r.at[k], to)

    def fany(k, back):
        to = (y_to[0], y_far, y_to[1])[k - 1]
        return remote(panel.at[2, 0, yy(-k * (1 - back))], fy_s.at[k], fy_r.at[k], to)

    def fanz(n, d, w):
        src = panel.at[2, slot(n, d - 1), w]
        dst = panel.at[2, slot(n, d), w]
        return both(src, dst, fz_s.at[n, d, w], fz_r.at[n, d, w], z_to[n])

    def ring_on(d):
        for n in range(2):
            ring(n, d).wait_recv()
            if d <= 6:
                ring(n, d + 2).start()

    def fanz_go(ws):
        for w in ws:
            for n in range(2):
                fanz(n, 1, w).start()

    def fanz_on(d, ws=(0, 1, 2, 3)):
        for w in ws:
            for n in range(2):
                if d < 8 or n == w // 2:
                    fanz(n, d, w).wait_recv()
                if d < 7 or (d == 7 and n == w // 2):
                    fanz(n, d + 1, w).start()

    own_coef(0).wait()
    got_coef(0).wait_recv()
    own_coef(1).wait()
    got_coef(1).wait_recv()
    for d in (1, 2):
        for n in range(2):
            ring(n, d).start()
    own_coef(2).wait()
    got_coef(2).wait_recv()
    for k in (1, 3, 2):
        fanx(k, 1).start()

    lane = lax.broadcasted_iota(jnp.int32, (32, 512), 1)
    row = lax.broadcasted_iota(jnp.int32, (32, 512), 0)
    get_starts.wait()
    get_order.wait()
    want = row % SHW
    for s in range(8):
        want = want + jnp.where(row // SHW == s, starts_ref[s], 0)

    def pick(q, carry):
        at = pl.multiple_of(q * 512, 512)
        rows[256:288, pl.ds(at, 512)] = jnp.where(lane + q * 512 == want, 1.0, 0.0).astype(BF16)
        return carry

    def spot(ch, m, l):
        return (l, m) if ch == 0 else (m, l)

    mid_to = (x_to, y_to)
    last_to = (y_to, x_to)
    here = (x, y)
    line = (y, x)

    def wrap(v, k):
        return (v + k + 4) % 4

    LOW = (0, 5, 9, 13)
    COUNT = (5, 4, 4, 3)

    def group(ch, g, y_, x_):
        return panel.at[ch, pl.ds(LOW[g], COUNT[g]), y_, x_]

    def group_half(ch, g, y_, x_, n):
        return panel.at[ch, pl.ds(LOW[g], COUNT[g]), y_, x_, pl.ds(16 * n, 16), :]

    def mid(ch, g, n, back):
        y_, x_ = spot(ch, wrap(here[ch], -SIGN[n] * (1 - back)), line[ch])
        return remote(group(ch, g, y_, x_), mid_s.at[ch, g, n], mid_r.at[ch, g, n], mid_to[ch][n])

    def midf(ch, g, n, back):
        y_, x_ = spot(ch, wrap(here[ch], -SIGN[n] * (2 - back)), line[ch])
        return remote(group_half(ch, g, y_, x_, n), midf_s.at[ch, g, n], midf_r.at[ch, g, n], mid_to[ch][n])

    def last(ch, g, k, n, back):
        y_, x_ = spot(ch, wrap(here[ch], k), wrap(line[ch], -SIGN[n] * (1 - back)))
        return remote(group(ch, g, y_, x_), last_s.at[ch, g, k, n], last_r.at[ch, g, k, n], last_to[ch][n])

    def lastf(ch, g, k, n, back):
        y_, x_ = spot(ch, wrap(here[ch], k), wrap(line[ch], -SIGN[n] * (2 - back)))
        return remote(group_half(ch, g, y_, x_, n), lastf_s.at[ch, g, k, n], lastf_r.at[ch, g, k, n],
                      last_to[ch][n])

    BOTH = [(ch, n) for ch in range(2) for n in range(2)]

    def p0(g):
        for ch, n in BOTH:
            mid(ch, g, n, 1).start()
        for ch, n in BOTH:
            last(ch, g, 0, n, 1).start()

    def p1(g):
        for ch, n in BOTH:
            mid(ch, g, n, 0).wait_recv()
            midf(ch, g, n, 1).start()
        for k in (1, 3):
            for ch, n in BOTH:
                last(ch, g, k, n, 1).start()

    def p2(g):
        for ch, n in BOTH:
            midf(ch, g, n, 0).wait_recv()
        for ch, n in BOTH:
            last(ch, g, 2, n, 1).start()

    def p3(g, *ks):
        for k in ks:
            for ch, n in BOTH:
                last(ch, g, k, n, 0).wait_recv()
                lastf(ch, g, k, n, 1).start()

    def columns(s):
        d = (s + 1) // 2
        o = (z + (1 - 2 * (s % 2)) * d + 32) % 16
        cuts = []
        for w in range(4):
            at = pl.multiple_of((((o % 4) * 4 + w) * 4 + o // 4) * 128, 128)
            cuts.append(rows[:, pl.ds(at, 128)])
        return jnp.concatenate(cuts, axis=1)

    def p4(g):
        for k in range(4):
            for ch, n in BOTH:
                lastf(ch, g, k, n, 0).wait_recv()

        def step(s, carry):
            block = jnp.concatenate([panel[0, s].reshape(512, 128), panel[1, s].reshape(512, 128)], axis=1)
            acc_ab[...] += jnp.dot(columns(s), block, preferred_element_type=F32)
            return carry

        lax.fori_loop(LOW[g], LOW[g] + COUNT[g], step, 0)

    def add_c(lo, hi):
        def step(s, carry):
            acc_c[...] += jnp.dot(columns(s), panel[2, s].reshape(512, 128), preferred_element_type=F32)
            return carry

        lax.fori_loop(lo, hi, step, 0)

    ring_on(1)
    for k in (1, 3, 2):
        fanx(k, 0).wait_recv()
    for k in (1, 3, 2):
        fany(k, 1).start()
    ring_on(2)
    p0(0)
    lax.fori_loop(0, 16, pick, 0)
    acc_ab[...] = jnp.zeros_like(acc_ab)
    acc_c[...] = jnp.zeros_like(acc_c)
    ring_on(3)
    ring_on(4)
    p0(1)
    for k in (1, 3, 2):
        fany(k, 0).wait_recv()
    fanz_go((0, 1))
    p1(0)
    ring_on(5)
    ring_on(6)
    p0(2)
    fanz_go((2, 3))
    p2(0)
    p1(1)
    fanz_on(1, (0, 1))
    ring_on(7)
    for n in range(2):
        ring(n, 8).wait_recv()
    p0(3)
    p3(0, 0)
    fanz_on(1, (2, 3))
    p2(1)
    p1(2)
    p3(1, 0)
    p3(0, 1, 3)
    fanz_on(2)
    p1(3)
    p2(2)
    p3(0, 2)
    p3(2, 0)
    p3(1, 1, 3)
    fanz_on(3)
    p2(3)
    p3(1, 2)
    p3(3, 0)
    p3(2, 1, 3)
    own_ints.wait()
    got_ints.wait_recv()
    fanz_on(4)
    p3(2, 2)
    p3(3, 1, 3)
    p4(0)
    fanz_on(5)
    p3(3, 2)
    p4(1)
    add_c(0, 7)
    fanz_on(6)
    p4(2)
    fanz_on(7)
    add_c(7, 13)

    def piece(j, c_, x_, h_):
        return half.at[j, c_, x_, h_]

    def part(j, c_, x_, h_, n):
        return half.at[j, c_, x_, h_, pl.ds(128 * n, 128), :]

    def hz(j, n, back):
        return remote(piece(j, c, x, hh(-SIGN[n] * (1 - back))), hz_s.at[j, n], hz_r.at[j, n], h_to[n])

    def hzf(j, n, back):
        return remote(part(j, c, x, hh(-SIGN[n] * (2 - back)), n), hzf_s.at[j, n], hzf_r.at[j, n], h_to[n])

    def hx(j, k, n, back):
        return remote(piece(j, c, xx(-SIGN[n] * (1 - back)), hh(k)), hx_s.at[j, k, n], hx_r.at[j, k, n], x_to[n])

    def hxf(j, k, n, back):
        return remote(part(j, c, xx(-SIGN[n] * (2 - back)), hh(k), n), hxf_s.at[j, k, n], hxf_r.at[j, k, n], x_to[n])

    def hp(j, xk, k, c_):
        return remote(piece(j, c_, xx(xk), hh(k)), hp_s.at[j, xk, k], hp_r.at[j, xk, k], partner)

    def save(j, v):
        half[j, c, x, zhi] = v[:256].astype(BF16)
        batch[c, :, 128 * j:128 * (j + 1)] = v[256:].astype(BF16)

    def spread(j, k):
        for n in range(2):
            hx(j, k, n, 1).start()
        hp(j, 0, k, c).start()

    def e0(j):
        for n in range(2):
            hz(j, n, 1).start()
        spread(j, 0)

    def e1(j):
        for n in range(2):
            hz(j, n, 0).wait_recv()
            hzf(j, n, 1).start()
        spread(j, 1)
        spread(j, 3)

    def e2(j):
        for n in range(2):
            hzf(j, n, 0).wait_recv()
        spread(j, 2)

    def x1(j, k):
        for n in range(2):
            hx(j, k, n, 0).wait_recv()
            hxf(j, k, n, 1).start()
        hp(j, 3, k, c).start()
        hp(j, 1, k, c).start()

    def x2(j, k):
        for n in range(2):
            hxf(j, k, n, 0).wait_recv()
        hp(j, 2, k, c).start()

    p4(3)
    save(0, acc_ab[:, 0:128])
    e0(0)
    save(1, acc_ab[:, 128:256])
    e0(1)
    fanz_on(8)
    add_c(13, 16)
    save(2, acc_c[...])
    swap = remote(batch.at[c], b_s.at[0], b_r.at[0], partner)
    swap.start()
    x1(0, 0)
    x1(1, 0)
    e1(0)
    e0(2)
    x2(0, 0)
    x2(1, 0)
    remote(batch.at[other], b_s.at[0], b_r.at[0], partner).wait_recv()

    r96 = lax.broadcasted_iota(jnp.int32, (96, 384), 0)
    c384 = lax.broadcasted_iota(jnp.int32, (96, 384), 1)
    chosen = jnp.where(c384 == p * 12 + r96 // 8, 1.0, 0.0).astype(BF16)
    r256 = lax.broadcasted_iota(jnp.int32, (96, 256), 0)
    c256 = lax.broadcasted_iota(jnp.int32, (96, 256), 1)
    same = r256 % 8 == c256 // 32
    grid = []
    for t in range(2):
        wide = jnp.concatenate([batch[t]] * 8, axis=0)
        g = lax.dot_general(chosen, wide, (((1,), (1,)), ((), ())), preferred_element_type=F32)
        grid.append(jnp.where(same, g, 0.0))
    mix[0:96, 0:256] = grid[0].astype(BF16)
    mix[0:96, 256:512] = grid[1].astype(BF16)
    mix[96:192, 0:256] = (-grid[1]).astype(BF16)
    mix[96:192, 256:512] = grid[0].astype(BF16)
    spots = lax.broadcasted_iota(jnp.int32, (128, 128), 0)
    select = jnp.transpose(jnp.where(spots == order_ref[0:1, :], 1.0, 0.0)).astype(BF16)

    def hp_wait(j, ks):
        for xk in range(4):
            for k in ks:
                hp(j, xk, k, other).wait_recv()

    def mixed(js, ks):
        lo, n = js[0], len(js)

        def one(t, carry):
            for k in ks:
                h_, x_ = hh(k), t
                v = jnp.zeros((192, 128 * n), F32)
                for t_ in range(2):
                    b = jnp.concatenate([half[j, t_, x_, h_] for j in js], axis=1)
                    v = v + jnp.dot(mix[:, 256 * t_:256 * (t_ + 1)], b, preferred_element_type=F32)
                at = pl.ds(pl.multiple_of((h_ * 4 + x_) * 8, 8), 8)
                for i, j in enumerate(js):
                    trans[j, :, at, :] = v[:, 128 * i:128 * (i + 1)].reshape(24, 8, 128)
            return carry

        lax.fori_loop(0, 4, one, 0)

    def turn(j):
        def some(t, carry):
            for u in range(4):
                v = jnp.transpose(trans[j, t * 4 + u]).astype(BF16)
                outv[t * 4 + u, 128 * j:128 * (j + 1), :] = jnp.dot(
                    v, select, preferred_element_type=F32).astype(BF16)
            return carry

        lax.fori_loop(0, 6, some, 0)

    e1(1)
    x1(2, 0)
    x1(0, 1)
    x1(0, 3)
    x1(1, 1)
    x1(1, 3)
    x2(0, 1)
    x2(0, 3)
    e1(2)
    hp_wait(0, (0,))
    hp_wait(1, (0,))
    mixed((0, 1), (0,))
    x2(1, 1)
    x2(1, 3)
    x2(2, 0)
    e2(0)
    x1(2, 1)
    x1(2, 3)
    e2(1)
    hp_wait(0, (1, 3))
    hp_wait(1, (1, 3))
    mixed((0, 1), (1, 3))
    x1(0, 2)
    x2(2, 1)
    x2(2, 3)
    x1(1, 2)
    e2(2)
    hp_wait(2, (0,))
    mixed((2,), (0,))
    x2(0, 2)
    x2(1, 2)
    x1(2, 2)
    hp_wait(0, (2,))
    hp_wait(1, (2,))
    mixed((0, 1), (2,))
    x2(2, 2)
    turn(0)
    def put(j):
        cols = pl.ds(128 * j, 128)
        return pltpu.make_async_copy(outv.at[:, cols, :], out_ref.at[:, cols, :], loc_sem.at[j])

    put(0).start()
    hp_wait(2, (1, 3))
    mixed((2,), (1, 3))
    turn(1)
    put(1).start()
    hp_wait(2, (2,))
    mixed((2,), (2,))
    turn(2)
    put(2).start()

    for j in range(3):
        give_coef(j).wait_send()
    give_ints.wait_send()
    swap.wait_send()
    for k in (1, 2, 3):
        fanx(k, 1).wait_send()
        fany(k, 1).wait_send()

    for n in range(2):
        for d in range(1, 9):
            ring(n, d).wait_send()
            for w in range(4):
                if d < 8 or n == w // 2:
                    fanz(n, d, w).wait_send()
    for n in range(2):
        for ch in range(2):
            for g in range(4):
                mid(ch, g, n, 1).wait_send()
                midf(ch, g, n, 1).wait_send()
                for k in range(4):
                    last(ch, g, k, n, 1).wait_send()
                    lastf(ch, g, k, n, 1).wait_send()
        for j in range(3):
            hz(j, n, 1).wait_send()
            hzf(j, n, 1).wait_send()
            for k in range(4):
                hx(j, k, n, 1).wait_send()
                hxf(j, k, n, 1).wait_send()
    for j in range(3):
        for xk in range(4):
            for k in range(4):
                hp(j, xk, k, c).wait_send()
    for j in range(3):
        put(j).wait()


def on_device(integrals, coefficients, shell_starts, pair_ids):
    slot_count, batch_rows, ao_width = integrals.shape
    ints = integrals.reshape(slot_count * batch_rows, ao_width)
    D = pltpu.SemaphoreType.DMA
    pairs = [(3,), (1,), (2, 9), (4,), (4,), (2, 9, 4), (2, 4, 2), (2, 4, 2), (2, 4, 4, 2), (2, 4, 4, 2),
             (1,), (3, 2), (3, 2), (3, 4, 2), (3, 4, 2), (3, 4, 4)]
    sems = [D((6,))]
    for shape in pairs:
        sems += [D(shape), D(shape)]
    out = pl.pallas_call(
        kernel,
        out_shape=jax.ShapeDtypeStruct((24, 384, 128), BF16),
        in_specs=[
            pl.BlockSpec(memory_space=pltpu.HBM),
            pl.BlockSpec(memory_space=pltpu.HBM),
            pl.BlockSpec(memory_space=pltpu.HBM),
            pl.BlockSpec(memory_space=pltpu.HBM),
        ],
        out_specs=pl.BlockSpec(memory_space=pl.ANY),
        scratch_shapes=[
            pltpu.SMEM((8,), jnp.int32),
            pltpu.VMEM((1, 128), jnp.int32),
            pltpu.VMEM((288, 8192), BF16),
            pltpu.VMEM((3, 16, 4, 4, 32, 128), BF16),
            pltpu.VMEM((3, 2, 4, 4, 256, 128), BF16),
            pltpu.VMEM((2, 32, 384), BF16),
            pltpu.VMEM((192, 512), BF16),
            pltpu.VMEM((3, 24, 128, 128), F32),
            pltpu.VMEM((24, 384, 128), BF16),
            pltpu.VMEM((288, 256), F32),
            pltpu.VMEM((288, 128), F32),
        ] + sems,
        compiler_params=pltpu.CompilerParams(
            collective_id=0, has_side_effects=True, vmem_limit_bytes=67043328),
    )(shell_starts, pair_ids, ints, coefficients)
    return out.reshape(2, 12, 384, 128)


def solution(mesh):
    return jax.shard_map(
        on_device,
        mesh=mesh,
        in_specs=(
            P(("coef", "pair"), None, None),
            P(None, ("coef", "pair"), None),
            P(),
            P("coef", None),
        ),
        out_specs=P(None, "pair", None, "coef"),
        check_vma=False,
    )
```

```python
import jax
import jax.numpy as jnp
from jax import lax
from jax.experimental import pallas as pl
from jax.experimental.pallas import tpu as pltpu
from jax.sharding import PartitionSpec as P

MESH = pl.DeviceIdType.MESH
SHW = 4
F32 = jnp.float32
BF16 = jnp.bfloat16


def kernel(starts_in, order_in, ints_ref, coef_ref, out_ref,
           starts_ref, order_ref, rows, panel, half, batch, mix, trans, outv, acc,
           loc_sem, cc_s, cc_r, ci_s, ci_r, ring_s, ring_r,
           mid_s, mid_r, midf_s, midf_r, last_s, last_r, lastf_s, lastf_r,
           b_s, b_r, hz_s, hz_r, hzf_s, hzf_r, hx_s, hx_r, hxf_s, hxf_r, hp_s, hp_r):
    a = lax.axis_index("coef")
    p = lax.axis_index("pair")
    zlo, y = a // 4, a % 4
    zhi, x, c = p // 8, (p // 2) % 4, p % 2
    z = zhi * 4 + zlo
    other = 1 - c

    def dev(z_, y_, x_, c_):
        return ((z_ % 4) * 4 + y_, (z_ // 4) * 8 + x_ * 2 + c_)

    def zz(k):
        return (z + k + 16) % 16

    def yy(k):
        return (y + k + 4) % 4

    def xx(k):
        return (x + k + 4) % 4

    def hh(k):
        return (zhi + k + 4) % 4

    partner = dev(z, y, x, other)
    z_to = (dev(zz(1), y, x, c), dev(zz(-1), y, x, c))
    z2_to = (dev(zz(2), y, x, c), dev(zz(-2), y, x, c))
    y_to = (dev(z, yy(1), x, c), dev(z, yy(-1), x, c))
    x_to = (dev(z, y, xx(1), c), dev(z, y, xx(-1), c))
    h_to = (dev(zz(4), y, x, c), dev(zz(-4), y, x, c))
    SIGN = (1, -1)

    def remote(ref, ssem, rsem, to):
        return pltpu.make_async_remote_copy(src_ref=ref, dst_ref=ref, send_sem=ssem, recv_sem=rsem,
                                            device_id=to, device_id_type=MESH)

    core_rows = pl.ds(pl.multiple_of(c * 16, 16), 16)
    int_rows = pl.ds(pl.multiple_of(c * 128, 128), 128)

    def own_coef(j):
        return pltpu.make_async_copy(coef_ref.at[c, :, pl.ds(128 * j, 128)],
                                     panel.at[j, 0, y, x, core_rows, :], loc_sem.at[j])

    own_ints = pltpu.make_async_copy(ints_ref, rows.at[int_rows, :], loc_sem.at[3])

    def give_coef(j):
        return pltpu.make_async_remote_copy(
            src_ref=coef_ref.at[other, :, pl.ds(128 * j, 128)],
            dst_ref=panel.at[j, 0, y, x, core_rows, :],
            send_sem=cc_s.at[j], recv_sem=cc_r.at[j], device_id=partner, device_id_type=MESH)

    def got_coef(j):
        ref = panel.at[j, 0, y, x, pl.ds(pl.multiple_of(other * 16, 16), 16), :]
        return remote(ref, cc_s.at[j], cc_r.at[j], partner)

    give_ints = pltpu.make_async_remote_copy(
        src_ref=ints_ref, dst_ref=rows.at[int_rows, :],
        send_sem=ci_s.at[0], recv_sem=ci_r.at[0], device_id=partner, device_id_type=MESH)
    got_ints = remote(rows.at[pl.ds(pl.multiple_of(other * 128, 128), 128), :], ci_s.at[0], ci_r.at[0], partner)

    for j in range(3):
        own_coef(j).start()
    own_ints.start()
    get_starts = pltpu.make_async_copy(starts_in, starts_ref, loc_sem.at[4])
    get_order = pltpu.make_async_copy(order_in, order_ref, loc_sem.at[5])
    get_starts.start()
    get_order.start()

    barrier = pltpu.get_barrier_semaphore()
    peers = (partner,) + z_to + z2_to + y_to + x_to + h_to
    for peer in peers:
        pl.semaphore_signal(barrier, inc=1, device_id=peer, device_id_type=MESH)
    pl.semaphore_wait(barrier, len(peers))

    for j in range(3):
        give_coef(j).start()
    give_ints.start()

    def slot(n, d):
        return 15 if d == 8 else (0 if d == 0 else 2 * d - 1 + n)

    def both(src, dst, ssem, rsem, to):
        return pltpu.make_async_remote_copy(src_ref=src, dst_ref=dst, send_sem=ssem, recv_sem=rsem,
                                            device_id=to, device_id_type=MESH)

    def ring(n, d):
        row_part = pl.ds(0, 32) if d < 8 else pl.ds(16 * n, 16)
        src = panel.at[:, slot(n, max(d - 2, 0)), y, x, row_part, :]
        dst = panel.at[:, slot(n, d), y, x, row_part, :]
        return both(src, dst, ring_s.at[n, d], ring_r.at[n, d], (z_to if d == 1 else z2_to)[n])

    def ring_on(d):
        for n in range(2):
            ring(n, d).wait_recv()
            if d <= 6:
                ring(n, d + 2).start()

    for j in range(3):
        own_coef(j).wait()
        got_coef(j).wait_recv()
    for d in (1, 2):
        for n in range(2):
            ring(n, d).start()

    lane = lax.broadcasted_iota(jnp.int32, (32, 512), 1)
    row = lax.broadcasted_iota(jnp.int32, (32, 512), 0)
    get_starts.wait()
    get_order.wait()
    want = row % SHW
    for s in range(8):
        want = want + jnp.where(row // SHW == s, starts_ref[s], 0)

    def pick(q, carry):
        at = pl.multiple_of(q * 512, 512)
        rows[256:288, pl.ds(at, 512)] = jnp.where(lane + q * 512 == want, 1.0, 0.0).astype(BF16)
        return carry

    def spot(ch, m, l):
        return (l, m) if ch == 0 else (m, l)

    mid_to = (x_to, y_to)
    last_to = (y_to, x_to)
    here = (x, y)
    line = (y, x)

    def wrap(v, k):
        return (v + k + 4) % 4

    UNIT = (
        (0, 5, (0, 1), (0, 1), True),
        (5, 4, (0, 1), (0, 1), True),
        (9, 4, (0, 1), (0, 1), True),
        (13, 3, (0, 1), (0, 1), True),
        (0, 8, (0, 1), (2, 2), False),
        (8, 8, (0, 1), (2, 2), False),
    )

    def span(ch, g, y_, x_, lo, count):
        _, _, routes, chunks, whole = UNIT[g]
        j = chunks[routes.index(ch)]
        if whole:
            return panel.at[j, pl.ds(lo, count), y_, x_]
        return panel.at[j, pl.ds(lo, count), y_, x_, pl.ds(16 * ch, 16), :]

    def group(ch, g, y_, x_):
        return span(ch, g, y_, x_, UNIT[g][0], UNIT[g][1])

    def group_half(ch, g, y_, x_, n):
        lo, count, routes, chunks, whole = UNIT[g]
        if whole:
            return panel.at[chunks[routes.index(ch)], pl.ds(lo, count), y_, x_, pl.ds(16 * n, 16), :]
        first = (count + 1) // 2
        return span(ch, g, y_, x_, lo + n * first, count - first if n else first)

    def mid(ch, g, n, back):
        y_, x_ = spot(ch, wrap(here[ch], -SIGN[n] * (1 - back)), line[ch])
        return remote(group(ch, g, y_, x_), mid_s.at[ch, g, n], mid_r.at[ch, g, n], mid_to[ch][n])

    def midf(ch, g, n, back):
        y_, x_ = spot(ch, wrap(here[ch], -SIGN[n] * (2 - back)), line[ch])
        return remote(group_half(ch, g, y_, x_, n), midf_s.at[ch, g, n], midf_r.at[ch, g, n], mid_to[ch][n])

    def last(ch, g, k, n, back):
        y_, x_ = spot(ch, wrap(here[ch], k), wrap(line[ch], -SIGN[n] * (1 - back)))
        return remote(group(ch, g, y_, x_), last_s.at[ch, g, k, n], last_r.at[ch, g, k, n], last_to[ch][n])

    def lastf(ch, g, k, n, back):
        y_, x_ = spot(ch, wrap(here[ch], k), wrap(line[ch], -SIGN[n] * (2 - back)))
        return remote(group_half(ch, g, y_, x_, n), lastf_s.at[ch, g, k, n], lastf_r.at[ch, g, k, n],
                      last_to[ch][n])

    def both_of(g):
        return [(ch, n) for ch in UNIT[g][2] for n in range(2)]

    def m0(*gs):
        for g in gs:
            for ch, n in both_of(g):
                mid(ch, g, n, 1).start()

    def l0(g):
        for ch, n in both_of(g):
            last(ch, g, 0, n, 1).start()

    def p1m(*gs):
        for g in gs:
            for ch, n in both_of(g):
                mid(ch, g, n, 0).wait_recv()
                midf(ch, g, n, 1).start()

    def p1l(g):
        for k in (1, 3):
            for ch, n in both_of(g):
                last(ch, g, k, n, 1).start()

    def p2(g):
        for ch, n in both_of(g):
            midf(ch, g, n, 0).wait_recv()
        for ch, n in both_of(g):
            last(ch, g, 2, n, 1).start()

    def p3(g, *ks):
        for k in ks:
            for ch, n in both_of(g):
                last(ch, g, k, n, 0).wait_recv()
                lastf(ch, g, k, n, 1).start()

    def columns(s):
        d = (s + 1) // 2
        o = (z + (1 - 2 * (s % 2)) * d + 32) % 16
        cuts = []
        for w in range(4):
            at = pl.multiple_of((((o % 4) * 4 + w) * 4 + o // 4) * 128, 128)
            cuts.append(rows[:, pl.ds(at, 128)])
        return jnp.concatenate(cuts, axis=1)

    def p4(g):
        for k in range(4):
            for ch, n in both_of(g):
                lastf(ch, g, k, n, 0).wait_recv()

        lo, count, _, chunks, _ = UNIT[g]
        js = tuple(sorted(set(chunks)))

        def step(s, carry):
            block = jnp.concatenate([panel[j, s].reshape(512, 128) for j in js], axis=1)
            v = jnp.dot(columns(s), block, preferred_element_type=F32)
            for i, j in enumerate(js):
                acc[j] += v[:, 128 * i:128 * (i + 1)]
            return carry

        lax.fori_loop(lo, lo + count, step, 0, unroll=2)

    def piece(j, c_, x_, h_):
        return half.at[j, c_, x_, h_]

    def part(j, c_, x_, h_, n):
        return half.at[j, c_, x_, h_, pl.ds(128 * n, 128), :]

    def hz(j, n, h, back):
        return remote(part(j, c, x, hh(-SIGN[n] * (1 - back)), h), hz_s.at[j, n, h], hz_r.at[j, n, h], h_to[n])

    def hzf(j, n, back):
        return remote(part(j, c, x, hh(-SIGN[n] * (2 - back)), n), hzf_s.at[j, n], hzf_r.at[j, n], h_to[n])

    def hx(j, k, n, back):
        return remote(piece(j, c, xx(-SIGN[n] * (1 - back)), hh(k)), hx_s.at[j, k, n], hx_r.at[j, k, n], x_to[n])

    def hxf(j, k, n, back):
        return remote(part(j, c, xx(-SIGN[n] * (2 - back)), hh(k), n), hxf_s.at[j, k, n], hxf_r.at[j, k, n], x_to[n])

    def hp(j, xk, k, c_):
        return remote(piece(j, c_, xx(xk), hh(k)), hp_s.at[j, xk, k], hp_r.at[j, xk, k], partner)

    def save(j):
        v = acc[j]
        half[j, c, x, zhi] = v[:256].astype(BF16)
        batch[c, :, 128 * j:128 * (j + 1)] = v[256:].astype(BF16)

    def spread(j, k):
        for n in range(2):
            hx(j, k, n, 1).start()
        hp(j, 0, k, c).start()

    def e0(j):
        for n in range(2):
            hz(j, n, n, 1).start()
        for n in range(2):
            hz(j, n, 1 - n, 1).start()
        spread(j, 0)

    def e1a(j):
        for n in range(2):
            hz(j, n, n, 0).wait_recv()
            hzf(j, n, 1).start()

    def e1b(j):
        for n in range(2):
            hz(j, n, 1 - n, 0).wait_recv()
        spread(j, 1)
        spread(j, 3)

    def e2(j):
        for n in range(2):
            hzf(j, n, 0).wait_recv()
        spread(j, 2)

    def x1(j, k):
        for n in range(2):
            hx(j, k, n, 0).wait_recv()
            hxf(j, k, n, 1).start()
        hp(j, 3, k, c).start()
        hp(j, 1, k, c).start()

    def x2(j, k):
        for n in range(2):
            hxf(j, k, n, 0).wait_recv()
        hp(j, 2, k, c).start()

    swap = remote(batch.at[c], b_s.at[0], b_r.at[0], partner)

    def blend():
        remote(batch.at[other], b_s.at[0], b_r.at[0], partner).wait_recv()
        r96 = lax.broadcasted_iota(jnp.int32, (96, 384), 0)
        c384 = lax.broadcasted_iota(jnp.int32, (96, 384), 1)
        chosen = jnp.where(c384 == p * 12 + r96 // 8, 1.0, 0.0).astype(BF16)
        r256 = lax.broadcasted_iota(jnp.int32, (96, 256), 0)
        c256 = lax.broadcasted_iota(jnp.int32, (96, 256), 1)
        same = r256 % 8 == c256 // 32
        grid = []
        for t in range(2):
            wide = jnp.concatenate([batch[t]] * 8, axis=0)
            g = lax.dot_general(chosen, wide, (((1,), (1,)), ((), ())), preferred_element_type=F32)
            grid.append(jnp.where(same, g, 0.0))
        mix[0:96, 0:256] = grid[0].astype(BF16)
        mix[0:96, 256:512] = grid[1].astype(BF16)
        mix[96:192, 0:256] = (-grid[1]).astype(BF16)
        mix[96:192, 256:512] = grid[0].astype(BF16)
        spots = lax.broadcasted_iota(jnp.int32, (128, 128), 0)
        select = jnp.transpose(jnp.where(spots == order_ref[0:1, :], 1.0, 0.0)).astype(BF16)
        return select

    def hp_wait(j, ks):
        for xk in range(4):
            for k in ks:
                hp(j, xk, k, other).wait_recv()

    def mixed(js, ks):
        n = len(js)

        for k in ks:
            h_ = hh(k)
            for x_ in range(4):
                v = jnp.zeros((192, 128 * n), F32)
                for t_ in range(2):
                    b = jnp.concatenate([half[j, t_, x_, h_] for j in js], axis=1)
                    v = v + jnp.dot(mix[:, 256 * t_:256 * (t_ + 1)], b, preferred_element_type=F32)
                at = pl.ds(pl.multiple_of((h_ * 4 + x_) * 8, 8), 8)
                for i, j in enumerate(js):
                    trans[j, :, at, :] = v[:, 128 * i:128 * (i + 1)].reshape(24, 8, 128)

    def turn(j, select):
        def some(t, carry):
            for u in range(4):
                v = jnp.transpose(trans[j, t * 4 + u]).astype(BF16)
                outv[t * 4 + u, 128 * j:128 * (j + 1), :] = jnp.dot(
                    v, select, preferred_element_type=F32).astype(BF16)
            return carry

        lax.fori_loop(0, 6, some, 0)

    def put(j):
        cols = pl.ds(128 * j, 128)
        return pltpu.make_async_copy(outv.at[:, cols, :], out_ref.at[:, cols, :], loc_sem.at[j])

    lax.fori_loop(0, 16, pick, 0)
    acc[...] = jnp.zeros_like(acc)
    ring_on(1)
    ring_on(2)
    m0(0)
    l0(0)
    ring_on(3)
    p1m(0)
    p1l(0)
    ring_on(4)
    l0(1)
    m0(1)
    p2(0)
    p3(0, 1)
    p3(0, 0)
    ring_on(5)
    ring_on(6)
    l0(2)
    m0(2)
    p1m(1)
    m0(4)
    p1l(1)
    ring_on(7)
    ring_on(8)
    m0(3)
    l0(3)
    p1m(2)
    p1l(2)
    p3(0, 2)
    p3(1, 0)
    p3(0, 3)
    p1m(3)
    p2(1)
    p2(2)
    p3(2, 0)
    p1l(3)
    p3(2, 1)
    p2(3)
    p3(1, 1)
    p3(2, 3)
    p3(1, 2)
    p3(2, 2)
    p3(1, 3)
    m0(5)
    p3(3, 0)
    p3(3, 3)
    own_ints.wait()
    got_ints.wait_recv()
    p4(0)
    p3(3, 2)
    p3(3, 1)
    p1m(4)
    p1l(4)
    l0(4)
    p4(2)
    p1m(5)
    p1l(5)
    p4(1)
    l0(5)
    p4(3)
    save(0)
    e0(0)
    p2(5)
    save(1)
    e0(1)
    p3(5, 1)
    p2(4)
    p3(5, 0)
    p3(5, 3)
    p3(5, 2)
    x1(0, 0)
    p3(4, 1)
    p3(4, 0)
    p3(4, 3)
    p3(4, 2)
    x1(1, 0)
    x2(0, 0)
    e1a(0)
    e1b(0)
    p4(5)
    p4(4)
    save(2)
    e0(2)
    x1(0, 1)
    e1a(1)
    e1b(1)
    e2(0)
    x1(1, 1)
    x1(0, 3)
    swap.start()
    x1(1, 3)
    e1a(2)
    x1(0, 2)
    select = blend()
    x1(2, 0)
    e1b(2)
    x2(0, 2)
    e2(1)
    hp_wait(0, (2,))
    mixed((0,), (2,))
    x2(1, 3)
    hp_wait(0, (0,))
    mixed((0,), (0,))
    x2(1, 0)
    x2(1, 1)
    x1(2, 1)
    x2(2, 0)
    e2(2)
    x2(0, 3)
    x2(0, 1)
    x1(2, 3)
    x1(1, 2)
    hp_wait(1, (3,))
    mixed((1,), (3,))
    hp_wait(0, (3,))
    mixed((0,), (3,))
    hp_wait(0, (1,))
    mixed((0,), (1,))
    turn(0, select)
    put(0).start()
    x1(2, 2)
    hp_wait(2, (0,))
    mixed((2,), (0,))
    x2(2, 1)
    hp_wait(1, (0,))
    mixed((1,), (0,))
    x2(2, 3)
    hp_wait(1, (1,))
    mixed((1,), (1,))
    x2(1, 2)
    hp_wait(2, (1,))
    mixed((2,), (1,))
    hp_wait(2, (3,))
    mixed((2,), (3,))
    hp_wait(1, (2,))
    mixed((1,), (2,))
    x2(2, 2)
    turn(1, select)
    put(1).start()
    hp_wait(2, (2,))
    mixed((2,), (2,))
    turn(2, select)
    put(2).start()

    for j in range(3):
        give_coef(j).wait_send()
    give_ints.wait_send()
    swap.wait_send()

    for n in range(2):
        for d in range(1, 9):
            ring(n, d).wait_send()
    for n in range(2):
        for g in range(6):
            for ch in UNIT[g][2]:
                mid(ch, g, n, 1).wait_send()
                midf(ch, g, n, 1).wait_send()
                for k in range(4):
                    last(ch, g, k, n, 1).wait_send()
                    lastf(ch, g, k, n, 1).wait_send()
        for j in range(3):
            hz(j, n, 0, 1).wait_send()
            hz(j, n, 1, 1).wait_send()
            hzf(j, n, 1).wait_send()
            for k in range(4):
                hx(j, k, n, 1).wait_send()
                hxf(j, k, n, 1).wait_send()
    for j in range(3):
        for xk in range(4):
            for k in range(4):
                hp(j, xk, k, c).wait_send()
    for j in range(3):
        put(j).wait()


def on_device(integrals, coefficients, shell_starts, pair_ids):
    slot_count, batch_rows, ao_width = integrals.shape
    ints = integrals.reshape(slot_count * batch_rows, ao_width)
    D = pltpu.SemaphoreType.DMA
    pairs = [(3,), (1,), (2, 9), (2, 6, 2), (2, 6, 2), (2, 6, 4, 2), (2, 6, 4, 2),
             (1,), (3, 2, 2), (3, 2), (3, 4, 2), (3, 4, 2), (3, 4, 4)]
    sems = [D((6,))]
    for shape in pairs:
        sems += [D(shape), D(shape)]
    out = pl.pallas_call(
        kernel,
        out_shape=jax.ShapeDtypeStruct((24, 384, 128), BF16),
        in_specs=[
            pl.BlockSpec(memory_space=pltpu.HBM),
            pl.BlockSpec(memory_space=pltpu.HBM),
            pl.BlockSpec(memory_space=pltpu.HBM),
            pl.BlockSpec(memory_space=pltpu.HBM),
        ],
        out_specs=pl.BlockSpec(memory_space=pl.ANY),
        scratch_shapes=[
            pltpu.SMEM((8,), jnp.int32),
            pltpu.VMEM((1, 128), jnp.int32),
            pltpu.VMEM((288, 8192), BF16),
            pltpu.VMEM((3, 16, 4, 4, 32, 128), BF16),
            pltpu.VMEM((3, 2, 4, 4, 256, 128), BF16),
            pltpu.VMEM((2, 32, 384), BF16),
            pltpu.VMEM((192, 512), BF16),
            pltpu.VMEM((3, 24, 128, 128), F32),
            pltpu.VMEM((24, 384, 128), BF16),
            pltpu.VMEM((3, 288, 128), F32),
        ] + sems,
        compiler_params=pltpu.CompilerParams(
            collective_id=0, has_side_effects=True, vmem_limit_bytes=40000000),
    )(*[pltpu.with_memory_space_constraint(v, pltpu.HBM) for v in (shell_starts, pair_ids, ints, coefficients)])
    return out.reshape(2, 12, 384, 128)


def solution(mesh):
    return jax.shard_map(
        on_device,
        mesh=mesh,
        in_specs=(
            P(("coef", "pair"), None, None),
            P(None, ("coef", "pair"), None),
            P(),
            P("coef", None),
        ),
        out_specs=P(None, "pair", None, "coef"),
        check_vma=False,
    )
```
